32 devices in a mesh: dp: 8 (over z, core), resp: 4 (over y, x).
Axes of the slice: x: 2, y: 2, z: 4, core: 2. Of those that a mesh axis runs over, the one named last changes fastest.
Arguments:
- queries: bfloat16 [8, 4, 128, 4096], P('dp', 'resp'), may hold values from -6 to 6
- prefix_kv: bfloat16 [8, 256, 1024], P('dp', 'resp'), may hold values from -6 to 6
- resp_kv: bfloat16 [8, 4, 128, 1024], P('dp', 'resp'), may hold values from -6 to 6
- direction: bfloat16 [8, 4, 128, 4096], P('dp', 'resp'), may hold values from -0.09375 to 0.09375
- base_logprob: float32 [8, 4, 128], P('dp', 'resp'), may hold values from -2 to 2
- rollout_logprob: float32 [8, 4, 128], P('dp', 'resp'), may hold values from -2 to 2
- destination: int32 [8, 4, 128], P('dp', 'resp'), may hold values from 0 to 1023, as said below
- advantage: float32 [8, 4], P('dp', 'resp'), may hold values from -4 to 4
- lengths: int32 [8, 4], P('dp', 'resp'), may hold values from 1 to 128, 384 in all within a row
- prefix_blocks: int32 [8, 4], P('dp', 'resp'), may hold values from 1 to 2, as said below
Outputs:
- query_grad: bfloat16 [8, 4, 128, 4096], P('dp', 'resp')
- resp_grad: bfloat16 [8, 4, 128, 1024], P('dp', 'resp')
- prefix_grad: bfloat16 [8, 256, 1024], P('dp', 'resp')
The draws below stay inside these ranges and needn't reach their ends.
Inputs may be any that keep to these rules, and one draw needn't show every extreme that they name: For each response index r, destination maps the 1024 rollout rows one to one onto the trainer rows; value g * 128 + t names token t of prompt group g; every index of dp holds exactly 16 rows bound for each prompt group. Each response sees the leading prefix_blocks blocks of 128 prompt rows; in every prompt group some response sees all 2. In every prompt group the lengths sum to 384 and one response has 128.
All inputs are finite; a program needn't handle non-finite values.
Results may differ from the reference program's by a relative error of at most 0.011.
Values may be sent and summed in bfloat16 or wider, within the bound.
A program may use at most 128 MiB of HBM per device.

```python
import math
import jax
import jax.numpy as jnp
import numpy as np
from jax import lax

QH = 32
KVH = 4
HD = 128
GQ = 8
BLOCK = 128
R = 128
P_SIZE = 256
PB = 2
GROUPS = 8
RESPS = 4


def draw_queries(key, part):
    shape = (GROUPS, RESPS, R, KVH, GQ, HD)
    values = jnp.clip(jax.random.normal(jax.random.fold_in(key, 1), shape, jnp.float32), -6.0, 6.0)
    return values.reshape(GROUPS, RESPS, R, QH * HD).astype(jnp.bfloat16)


def draw_prefix_kv(key, part):
    shape = (GROUPS, P_SIZE, 2, KVH, HD)
    values = jnp.clip(jax.random.normal(jax.random.fold_in(key, 2), shape, jnp.float32), -6.0, 6.0)
    return values.reshape(GROUPS, P_SIZE, 2 * KVH * HD).astype(jnp.bfloat16)


def draw_destination(key, part):
    per_peer = R // GROUPS
    target_keys = jax.random.split(jax.random.fold_in(key, 3), RESPS * GROUPS)
    target_perm = jax.vmap(lambda single: jax.random.permutation(single, R))(target_keys).astype(jnp.int32)
    target_perm = target_perm.reshape(RESPS, GROUPS, GROUPS, per_peer)
    offsets = (jnp.arange(GROUPS, dtype=jnp.int32) * R)[None, :, None, None]
    by_source = (target_perm + offsets).transpose(0, 2, 1, 3).reshape(RESPS, GROUPS, R)
    source_keys = jax.random.split(jax.random.fold_in(key, 4), RESPS * GROUPS)
    source_perm = jax.vmap(lambda single: jax.random.permutation(single, R))(source_keys).astype(jnp.int32)
    shuffled = jnp.take_along_axis(by_source, source_perm.reshape(RESPS, GROUPS, R), axis=2)
    return shuffled.transpose(1, 0, 2).astype(jnp.int32)


def draw_prefix_blocks(key, part):
    counts = jax.random.randint(jax.random.fold_in(key, 17), (GROUPS, RESPS), 1, PB + 1)
    full_view = jax.random.randint(jax.random.fold_in(key, 23), (GROUPS, 1), 0, RESPS)
    return jnp.where(jnp.arange(RESPS)[None, :] == full_view, PB, counts).astype(jnp.int32)


def levels(key, dims, pieces, low, high):
    def one(position, shards_of):
        heights = jax.random.uniform(jax.random.fold_in(jax.random.fold_in(key, 6), position), (shards_of,), jnp.float32, low / len(pieces), high / len(pieces))
        return jnp.repeat(jnp.exp(heights), dims[position] // shards_of).reshape((-1,) + (1,) * (len(dims) - position - 1))

    gain = one(*pieces[0])
    for cut in pieces[1:]:
        gain = gain * one(*cut)
    return gain


def split_up(number_of, total, most, slope):
    weights = [(1 << 20) // math.isqrt(grade ** slope) + 1 for grade in range(2, number_of + 1)]
    rest, given = total - most - (number_of - 1), [1] * (number_of - 1)
    while rest > 0:
        free = [i for i in range(number_of - 1) if given[i] < most]
        pool, left = sum([weights[i] for i in free]), rest
        for i in free:
            addition = min(most - given[i], max(1, left * weights[i] // pool), rest)
            given[i] = given[i] + addition
            rest = rest - addition
    return np.array([most] + given)


def uneven_parts(rng, amount, total, most, slope):
    if amount == 2:
        one = jax.random.randint(rng, (), max(1, total - most), min(most, total - 1) + 1)
        return jnp.stack([one, total - one])
    sizes = jnp.asarray(split_up(amount, total, most, slope), jnp.int32)
    couples = (amount - 1) // 2
    donor, taker = sizes[1:1 + 2 * couples:2], sizes[2:2 + 2 * couples:2]
    room = jnp.minimum(donor - 1, most - taker)
    passed = jax.random.randint(jax.random.fold_in(rng, 1), (couples,), 0, 1 << 20) % (room + 1)
    sizes = sizes.at[1:1 + 2 * couples:2].set(donor - passed).at[2:2 + 2 * couples:2].set(taker + passed)
    return sizes[jax.random.permutation(jax.random.fold_in(rng, 2), amount)]


def noise(own_key, shape, width, most, cuts=(), kind=jnp.bfloat16):
    factor_of = levels(own_key, shape, cuts, -0.22, 0.18) if cuts else 1.0
    entries = jax.random.normal(own_key, shape, jnp.float32) * width * factor_of
    return jnp.minimum(jnp.maximum(entries, -most), most).astype(kind)


def setup_inputs(seed: int = 0) -> dict:
    key_list = jax.random.split(jax.random.key(seed), 11)
    return {
        "queries": draw_queries(jax.random.fold_in(key_list[10], 71), 0),
        "prefix_kv": draw_prefix_kv(jax.random.fold_in(key_list[10], 71), 0),
        "resp_kv": noise(key_list[2], (GROUPS, RESPS, R, 2 * KVH * HD), 1.0, 6.0, ((0, 8), (1, 4))),
        "direction": noise(key_list[3], (GROUPS, RESPS, R, QH * HD), (QH * HD) ** -0.5, 0.09375, ((0, 8), (1, 4))),
        "base_logprob": noise(key_list[4], (GROUPS, RESPS, R), 0.25, 2.0, ((0, 8), (1, 4)), jnp.float32),
        "rollout_logprob": noise(key_list[5], (GROUPS, RESPS, R), 0.25, 2.0, ((0, 8), (1, 4)), jnp.float32),
        "destination": draw_destination(jax.random.fold_in(key_list[10], 71), 0),
        "advantage": noise(key_list[7], (GROUPS, RESPS), 1.0, 4.0, ((0, 8), (1, 4)), jnp.float32),
        "lengths": jax.vmap(lambda own: uneven_parts(own, RESPS, RESPS * R * 3 // 4, R, 1))(jax.random.split(key_list[8], GROUPS)).reshape((GROUPS, RESPS)).astype(jnp.int32),
        "prefix_blocks": draw_prefix_blocks(jax.random.fold_in(key_list[10], 71), 0),
    }


loss_scale = 65536.0
clip_lower = 0.8
clip_upper = 1.28

def one_response(queries_one, keys_values, direction_rows, base_rows, old_rows, advantage_one, length_one, blocks_one):
    tok_rows = queries_one.shape[0]
    total_keys = keys_values.shape[0]
    prefix_rows = total_keys - tok_rows
    score_scale = 1.0 / math.sqrt(HD)
    key_heads = keys_values[:, :KVH * HD].reshape(total_keys, KVH, HD).astype(jnp.float32)
    value_heads = keys_values[:, KVH * HD:].reshape(total_keys, KVH, HD).astype(jnp.float32)
    query_heads = queries_one.reshape(tok_rows, KVH, GQ, HD).astype(jnp.float32)
    key_index = jnp.arange(total_keys, dtype=jnp.int32)
    query_index = jnp.arange(tok_rows, dtype=jnp.int32)
    in_prefix = (key_index < prefix_rows) & (key_index // BLOCK < blocks_one)
    in_response = (key_index[None, :] >= prefix_rows) & (key_index[None, :] - prefix_rows <= query_index[:, None])
    allowed = in_prefix[None, :] | in_response
    scores = jnp.einsum('rhgd,lhd->hgrl', query_heads, key_heads) * score_scale
    scores = jnp.where(allowed[None, None], scores, -1e+30)
    shifted = jnp.exp(scores - lax.optimization_barrier(jnp.max(scores, axis=-1, keepdims=True)))
    prob_bf16 = (shifted / lax.optimization_barrier(jnp.sum(shifted, axis=-1, keepdims=True))).astype(jnp.bfloat16)
    prob_wide = lax.optimization_barrier(prob_bf16).astype(jnp.float32)
    attn_out = jnp.einsum('hgrl,lhd->rhgd', prob_wide, value_heads)
    out_bf16 = attn_out.reshape(tok_rows, QH * HD).astype(jnp.bfloat16)
    out_wide = lax.optimization_barrier(out_bf16).astype(jnp.float32)
    new_logprob = base_rows + lax.optimization_barrier(jnp.sum(out_wide * direction_rows.astype(jnp.float32), axis=-1))
    ratio_weight = jnp.clip(jnp.exp(new_logprob - old_rows), clip_lower, clip_upper)
    loss_coeff = jnp.where(query_index < length_one, -loss_scale * ratio_weight * advantage_one / length_one.astype(jnp.float32), 0.0)
    grad_out = (loss_coeff[:, None] * direction_rows.astype(jnp.float32)).astype(jnp.bfloat16)
    grad_heads = lax.optimization_barrier(grad_out).astype(jnp.float32).reshape(tok_rows, KVH, GQ, HD)
    prob_grad = jnp.einsum('rhgd,lhd->hgrl', grad_heads, value_heads)
    row_delta = lax.optimization_barrier(jnp.sum(grad_heads * attn_out, axis=-1)).transpose(1, 2, 0)
    dscore = (prob_wide * (prob_grad - row_delta[..., None]) * score_scale).astype(jnp.bfloat16)
    dscore_wide = lax.optimization_barrier(dscore).astype(jnp.float32)
    query_grad = jnp.einsum('hgrl,lhd->rhgd', dscore_wide, key_heads).reshape(tok_rows, QH * HD).astype(jnp.bfloat16)
    key_grad = jnp.einsum('hgrl,rhgd->lhd', dscore_wide, query_heads).reshape(total_keys, KVH * HD)
    value_grad = jnp.einsum('hgrl,rhgd->lhd', prob_wide, grad_heads).reshape(total_keys, KVH * HD)
    kv_grad = jnp.concatenate([key_grad, value_grad], axis=1)
    return (query_grad, kv_grad[prefix_rows:].astype(jnp.bfloat16), kv_grad[:prefix_rows])

def place_column(where_to, values):
    return jnp.zeros((GROUPS * R,), jnp.float32).at[where_to].set(values)

def reference(queries, prefix_kv, resp_kv, direction, base_logprob, rollout_logprob, destination, advantage, lengths, prefix_blocks):
    flat_dest = destination.transpose(1, 0, 2).reshape(RESPS, GROUPS * R)
    flat_old = rollout_logprob.transpose(1, 0, 2).reshape(RESPS, GROUPS * R)
    placed = jax.vmap(place_column)(flat_dest, flat_old)
    old_logprob = placed.reshape(RESPS, GROUPS, R).transpose(1, 0, 2)

    def per_group(group_inputs):
        query_group, prefix_group, resp_group, dir_group, base_group, old_group, adv_group, len_group, block_group = group_inputs

        def per_response(running_sum, response_inputs):
            query_one, resp_one, dir_one, base_one, old_one, adv_one, len_one, block_one = response_inputs
            keys_values = jnp.concatenate([prefix_group, resp_one], axis=0)
            query_grad, resp_grad, prefix_term = one_response(query_one, keys_values, dir_one, base_one, old_one, adv_one, len_one, block_one)
            return (running_sum + prefix_term, (query_grad, resp_grad))
        prefix_total, (query_grads, resp_grads) = lax.scan(per_response, jnp.zeros((P_SIZE, 2 * KVH * HD), jnp.float32), (query_group, resp_group, dir_group, base_group, old_group, adv_group, len_group, block_group))
        return (query_grads, resp_grads, prefix_total.astype(jnp.bfloat16))
    query_grad, resp_grad, prefix_grad = lax.map(per_group, (queries, prefix_kv, resp_kv, direction, base_logprob, old_logprob, advantage, lengths, prefix_blocks))
    return (query_grad, resp_grad, prefix_grad)
```

```python
import functools
import math

import jax
import jax.numpy as jnp
from jax import lax
from jax.experimental import pallas as pl
from jax.experimental.pallas import tpu as pltpu
from jax.sharding import PartitionSpec as P

QH = 32
KVH = 4
HD = 128
GQ = 8
BLOCK = 128
PAIR = 2

loss_scale = 65536.0
clip_lower = 0.8
clip_upper = 1.28

MESH = pl.DeviceIdType.MESH


def dot(a, b, dims):
    return lax.dot_general(a, b, (dims, ((), ())), preferred_element_type=jnp.float32)


def kernel(
    n_dp,
    n_resp,
    queries_hbm,
    prefix_hbm,
    resp_hbm,
    direction_hbm,
    base_ref,
    rollout_ref,
    destination_ref,
    advantage_ref,
    lengths_ref,
    blocks_ref,
    query_grad_hbm,
    resp_grad_hbm,
    prefix_grad_hbm,
    q_ref,
    d_ref,
    kv_ref,
    prob_ref,
    core_ref,
    bias_ref,
    qg_ref,
    rg_ref,
    pg_ref,
    row_send,
    row_recv,
    part_send,
    part_recv,
    load_sems,
    own_sems,
    prefix_send_sems,
    prefix_recv_sems,
    row_send_sems,
    row_recv_sems,
    part_send_sems,
    part_recv_sems,
    out_sems,
):
    my_dp, my_resp = lax.axis_index("dp"), lax.axis_index("resp")
    tok = q_ref.shape[0]
    shard = prefix_hbm.shape[0]
    total = kv_ref.shape[0]
    prefix_rows = total - tok
    width = GQ * HD
    score_scale = 1.0 / math.sqrt(HD)

    def head_cols(h):
        return pl.ds(pl.multiple_of(h * width, width), width)

    def kv_cols(h, x):
        return pl.ds(pl.multiple_of((x * KVH + h) * HD, HD), HD)

    def load_copies(h):
        return (
            pltpu.make_async_copy(
                queries_hbm.at[:, head_cols(h)], q_ref.at[:, head_cols(h)], load_sems.at[h, 0]
            ),
            pltpu.make_async_copy(
                direction_hbm.at[:, head_cols(h)], d_ref.at[:, head_cols(h)], load_sems.at[h, 1]
            ),
        )

    def shard_rows(owner):
        return pl.ds(pl.multiple_of(owner * shard, shard), shard)

    own_copies = (
        pltpu.make_async_copy(
            resp_hbm, kv_ref.at[pl.ds(prefix_rows, tok), :], own_sems.at[0]
        ),
        pltpu.make_async_copy(prefix_hbm, kv_ref.at[shard_rows(my_resp), :], own_sems.at[1]),
    )

    def resp_peer(k):
        return (my_dp, lax.rem(my_resp + k, n_resp))

    def dp_peer(k):
        return (lax.rem(my_dp + k, n_dp), my_resp)

    def prefix_copy(k, h, x, owner):
        return pltpu.make_async_remote_copy(
            src_ref=prefix_hbm.at[:, kv_cols(h, x)],
            dst_ref=kv_ref.at[shard_rows(owner), kv_cols(h, x)],
            send_sem=prefix_send_sems.at[k - 1, h, x],
            recv_sem=prefix_recv_sems.at[k - 1, h, x],
            device_id=resp_peer(k),
            device_id_type=MESH,
        )

    def row_copy(k):
        return pltpu.make_async_remote_copy(
            src_ref=row_send,
            dst_ref=row_recv.at[k - 1],
            send_sem=row_send_sems.at[k - 1],
            recv_sem=row_recv_sems.at[k - 1],
            device_id=dp_peer(k),
            device_id_type=MESH,
        )

    def part_copy(k, h):
        return pltpu.make_async_remote_copy(
            src_ref=part_send.at[h, lax.rem(my_resp + k, n_resp)],
            dst_ref=part_recv.at[k - 1, h],
            send_sem=part_send_sems.at[k - 1, h],
            recv_sem=part_recv_sems.at[k - 1, h],
            device_id=resp_peer(k),
            device_id_type=MESH,
        )

    barrier = pltpu.get_barrier_semaphore()
    for k in range(1, n_resp):
        pl.semaphore_signal(barrier, inc=1, device_id=resp_peer(k), device_id_type=MESH)
    for k in range(1, n_dp):
        pl.semaphore_signal(barrier, inc=1, device_id=dp_peer(k), device_id_type=MESH)
    for copy in own_copies:
        copy.start()
    for h in range(KVH):
        for copy in load_copies(h):
            copy.start()

    row_send[...] = jnp.zeros_like(row_send)
    row_send[0:1, :] = rollout_ref[...]
    row_send[1:2, :] = destination_ref[...].astype(jnp.float32)
    key_index = lax.broadcasted_iota(jnp.int32, (total, tok), 0)
    query_index = lax.broadcasted_iota(jnp.int32, (total, tok), 1)
    allowed = ((key_index < prefix_rows) & (key_index < blocks_ref[0, 0] * BLOCK)) | (
        (key_index >= prefix_rows) & (key_index - prefix_rows <= query_index)
    )
    bias_ref[...] = jnp.where(allowed, 0.0, -1e30)

    pl.semaphore_wait(barrier, n_resp - 1 + n_dp - 1)
    for h in range(KVH):
        for k in range(1, n_resp):
            for x in range(2):
                prefix_copy(k, h, x, my_resp).start()
    for k in range(1, n_dp):
        row_copy(k).start()
    for copy in own_copies:
        copy.wait()

    def forward(h, gained):
        for copy in load_copies(h):
            copy.wait()
        for k in range(1, n_resp):
            for x in range(2):
                prefix_copy(k, h, x, lax.rem(my_resp + n_resp - k, n_resp)).wait_recv()
        keys = kv_ref[:, kv_cols(h, 0)]
        values = kv_ref[:, kv_cols(h, 1)]
        bias = jnp.concatenate([bias_ref[...]] * PAIR, axis=1)
        for g in range(0, GQ, PAIR):
            starts = [pl.multiple_of(h * width + (g + i) * HD, HD) for i in range(PAIR)]
            q_rows = jnp.concatenate([q_ref[:, pl.ds(s, HD)] for s in starts], axis=0)
            d_rows = jnp.concatenate([d_ref[:, pl.ds(s, HD)] for s in starts], axis=0)
            scores = dot(keys, q_rows, ((1,), (1,))) * (score_scale * math.log2(math.e)) + bias
            shifted = jnp.exp2(scores - jnp.max(scores, axis=0, keepdims=True))
            inverse = 1.0 / jnp.sum(shifted, axis=0, keepdims=True)
            prob = (shifted * inverse).astype(jnp.bfloat16)
            wide = prob.astype(jnp.float32)
            toward = dot(values, d_rows, ((1,), (1,)))
            delta = jnp.sum(wide * toward, axis=0, keepdims=True)
            cols = pl.ds(g * HD, PAIR * HD)
            prob_ref[h, :, cols] = prob
            core_ref[h, :, cols] = (wide * (toward - delta)).astype(jnp.bfloat16)
            for i in range(PAIR):
                gained = gained + delta[:, i * HD : (i + 1) * HD]
        return gained

    gained = lax.fori_loop(0, KVH, forward, jnp.zeros((1, tok), jnp.float32))

    slot = (lax.broadcasted_iota(jnp.int32, (tok, tok), 0) + my_dp * tok).astype(jnp.float32)
    placed = jnp.where(row_send[1:2, :] == slot, row_send[0:1, :], 0.0)
    for k in range(1, n_dp):
        row_copy(k).wait_recv()
        placed = placed + jnp.where(
            row_recv[k - 1, 1:2, :] == slot, row_recv[k - 1, 0:1, :], 0.0
        )
    old = jnp.sum(placed.T, axis=0, keepdims=True)
    ratio = jnp.clip(jnp.exp(base_ref[...] + gained - old), clip_lower, clip_upper)
    length = lengths_ref[0, 0]
    coeff = jnp.where(
        lax.broadcasted_iota(jnp.int32, (1, tok), 1) < length,
        (-loss_scale * ratio) * advantage_ref[0, 0] / length.astype(jnp.float32),
        0.0,
    )
    coeff_rows = jnp.broadcast_to(coeff, (tok, tok)).T

    def kv_backward(h, carry):
        starts = [pl.multiple_of(h * width + g * HD, HD) for g in range(GQ)]
        for x, source, weights, factor in (
            (0, q_ref, core_ref, coeff_rows * score_scale),
            (1, d_ref, prob_ref, coeff_rows),
        ):
            rows = jnp.concatenate(
                [
                    (source[:, pl.ds(s, HD)].astype(jnp.float32) * factor).astype(jnp.bfloat16)
                    for s in starts
                ],
                axis=0,
            )
            grad = dot(weights[h], rows, ((1,), (0,))).astype(jnp.bfloat16)
            for owner in range(n_resp):
                part_send[h, owner, x] = grad[owner * shard : (owner + 1) * shard]
            rg_ref[:, kv_cols(h, x)] = grad[prefix_rows:]
        for k in range(1, n_resp):
            part_copy(k, h).start()
        return carry

    lax.fori_loop(0, KVH, kv_backward, 0)
    resp_out = pltpu.make_async_copy(rg_ref, resp_grad_hbm, out_sems.at[KVH])
    resp_out.start()

    def query_out(h):
        return pltpu.make_async_copy(
            qg_ref.at[:, head_cols(h)], query_grad_hbm.at[:, head_cols(h)], out_sems.at[h]
        )

    def query_backward(h, carry):
        grad = dot(kv_ref[:, kv_cols(h, 0)], core_ref[h], ((0,), (0,)))
        for g in range(GQ):
            one = grad[:, g * HD : (g + 1) * HD] * (coeff * score_scale)
            start = pl.multiple_of(h * width + g * HD, HD)
            qg_ref[:, pl.ds(start, HD)] = one.T.astype(jnp.bfloat16)
        query_out(h).start()
        return carry

    lax.fori_loop(0, KVH, query_backward, 0)

    for h in range(KVH):
        for k in range(1, n_resp):
            part_copy(k, h).wait_recv()
        for x in range(2):
            summed = part_send[h, my_resp, x].astype(jnp.float32)
            for k in range(1, n_resp):
                summed = summed + part_recv[k - 1, h, x].astype(jnp.float32)
            pg_ref[:, kv_cols(h, x)] = summed.astype(jnp.bfloat16)
    prefix_out = pltpu.make_async_copy(pg_ref, prefix_grad_hbm, out_sems.at[KVH + 1])
    prefix_out.start()

    for k in range(1, n_dp):
        row_copy(k).wait_send()
    for h in range(KVH):
        for k in range(1, n_resp):
            for x in range(2):
                prefix_copy(k, h, x, my_resp).wait_send()
            part_copy(k, h).wait_send()
        query_out(h).wait()
    resp_out.wait()
    prefix_out.wait()


def body(
    queries,
    prefix_kv,
    resp_kv,
    direction,
    base_logprob,
    rollout_logprob,
    destination,
    advantage,
    lengths,
    prefix_blocks,
):
    n_dp, n_resp = lax.axis_size("dp"), lax.axis_size("resp")
    tok = queries.shape[2]
    shard, kv_width = prefix_kv.shape[1:]
    total = n_resp * shard + tok
    columns = QH * HD
    any_spec = pl.BlockSpec(memory_space=pl.ANY)
    vmem_spec = pl.BlockSpec(memory_space=pltpu.VMEM)
    smem_spec = pl.BlockSpec(memory_space=pltpu.SMEM)
    dma = pltpu.SemaphoreType.DMA
    bf16, f32 = jnp.bfloat16, jnp.float32
    query_grad, resp_grad, prefix_grad = pl.pallas_call(
        functools.partial(kernel, n_dp, n_resp),
        out_shape=(
            jax.ShapeDtypeStruct((tok, columns), bf16),
            jax.ShapeDtypeStruct((tok, kv_width), bf16),
            jax.ShapeDtypeStruct((shard, kv_width), bf16),
        ),
        in_specs=[any_spec] * 4 + [vmem_spec] * 3 + [smem_spec] * 3,
        out_specs=(any_spec, any_spec, any_spec),
        scratch_shapes=[
            pltpu.VMEM((tok, columns), bf16),
            pltpu.VMEM((tok, columns), bf16),
            pltpu.VMEM((total, kv_width), bf16),
            pltpu.VMEM((KVH, total, GQ * tok), bf16),
            pltpu.VMEM((KVH, total, GQ * tok), bf16),
            pltpu.VMEM((total, tok), f32),
            pltpu.VMEM((tok, columns), bf16),
            pltpu.VMEM((tok, kv_width), bf16),
            pltpu.VMEM((shard, kv_width), bf16),
            pltpu.VMEM((8, tok), f32),
            pltpu.VMEM((n_dp - 1, 8, tok), f32),
            pltpu.VMEM((KVH, n_resp, 2, shard, HD), bf16),
            pltpu.VMEM((n_resp - 1, KVH, 2, shard, HD), bf16),
            dma((KVH, 2)),
            dma((2,)),
            dma((n_resp - 1, KVH, 2)),
            dma((n_resp - 1, KVH, 2)),
            dma((n_dp - 1,)),
            dma((n_dp - 1,)),
            dma((n_resp - 1, KVH)),
            dma((n_resp - 1, KVH)),
            dma((KVH + 2,)),
        ],
        compiler_params=pltpu.CompilerParams(
            collective_id=0, has_side_effects=True, vmem_limit_bytes=56 << 20
        ),
    )(
        queries[0, 0],
        prefix_kv[0],
        resp_kv[0, 0],
        direction[0, 0],
        base_logprob[0],
        rollout_logprob[0],
        destination[0],
        advantage,
        lengths,
        prefix_blocks,
    )
    return query_grad[None, None], resp_grad[None, None], prefix_grad[None]


def solution(mesh):
    return jax.shard_map(
        body,
        mesh=mesh,
        in_specs=(
            P("dp", "resp", None, None),
            P("dp", "resp", None),
            P("dp", "resp", None, None),
            P("dp", "resp", None, None),
            P("dp", "resp", None),
            P("dp", "resp", None),
            P("dp", "resp", None),
            P("dp", "resp"),
            P("dp", "resp"),
            P("dp", "resp"),
        ),
        out_specs=(P("dp", "resp", None, None), P("dp", "resp", None, None), P("dp", "resp", None)),
        check_vma=False,
    )
```

```python
import functools
import math

import jax
import jax.numpy as jnp
from jax import lax
from jax.experimental import pallas as pl
from jax.experimental.pallas import tpu as pltpu
from jax.sharding import PartitionSpec as P

QH = 32
KVH = 4
HD = 128
GQ = 8
BLOCK = 128
PAIR = 2

loss_scale = 65536.0
clip_lower = 0.8
clip_upper = 1.28

MESH = pl.DeviceIdType.MESH


def dot(a, b, dims):
    return lax.dot_general(a, b, (dims, ((), ())), preferred_element_type=jnp.float32)


def kernel(
    n_dp,
    n_resp,
    queries_hbm,
    prefix_hbm,
    resp_hbm,
    direction_hbm,
    base_hbm,
    rollout_hbm,
    destination_hbm,
    advantage_ref,
    lengths_ref,
    blocks_ref,
    qg_ref,
    rg_ref,
    pg_ref,
    q_ref,
    d_ref,
    kv_ref,
    prob_ref,
    core_ref,
    bias_ref,
    row_send,
    row_recv,
    part_send,
    part_recv,
    load_sems,
    own_sems,
    prefix_send_sems,
    prefix_recv_sems,
    row_send_sems,
    row_recv_sems,
    part_send_sems,
    part_recv_sems,
    base_ref,
    rollout_ref,
    destination_ref,
    small_sems,
):
    my_dp, my_resp = lax.axis_index("dp"), lax.axis_index("resp")
    tok = q_ref.shape[0]
    shard = prefix_hbm.shape[0]
    total = kv_ref.shape[0]
    prefix_rows = total - tok
    width = GQ * HD
    score_scale = 1.0 / math.sqrt(HD)

    def head_cols(h):
        return pl.ds(pl.multiple_of(h * width, width), width)

    def kv_cols(h, x):
        return pl.ds(pl.multiple_of((x * KVH + h) * HD, HD), HD)

    def load_copies(h):
        return (
            pltpu.make_async_copy(
                queries_hbm.at[:, head_cols(h)], q_ref.at[:, head_cols(h)], load_sems.at[h, 0]
            ),
            pltpu.make_async_copy(
                direction_hbm.at[:, head_cols(h)], d_ref.at[:, head_cols(h)], load_sems.at[h, 1]
            ),
        )

    def shard_rows(owner):
        return pl.ds(pl.multiple_of(owner * shard, shard), shard)

    own_copies = (
        pltpu.make_async_copy(
            resp_hbm, kv_ref.at[pl.ds(prefix_rows, tok), :], own_sems.at[0]
        ),
        pltpu.make_async_copy(prefix_hbm, kv_ref.at[shard_rows(my_resp), :], own_sems.at[1]),
    )

    def resp_peer(k):
        return (my_dp, lax.rem(my_resp + k, n_resp))

    def dp_peer(k):
        return (lax.rem(my_dp + k, n_dp), my_resp)

    def prefix_copy(k, h, x, owner):
        return pltpu.make_async_remote_copy(
            src_ref=prefix_hbm.at[:, kv_cols(h, x)],
            dst_ref=kv_ref.at[shard_rows(owner), kv_cols(h, x)],
            send_sem=prefix_send_sems.at[k - 1, h, x],
            recv_sem=prefix_recv_sems.at[k - 1, h, x],
            device_id=resp_peer(k),
            device_id_type=MESH,
        )

    def row_copy(k):
        return pltpu.make_async_remote_copy(
            src_ref=row_send,
            dst_ref=row_recv.at[k - 1],
            send_sem=row_send_sems.at[k - 1],
            recv_sem=row_recv_sems.at[k - 1],
            device_id=dp_peer(k),
            device_id_type=MESH,
        )

    def part_copy(k, h):
        return pltpu.make_async_remote_copy(
            src_ref=part_send.at[h, lax.rem(my_resp + k, n_resp)],
            dst_ref=part_recv.at[k - 1, h],
            send_sem=part_send_sems.at[k - 1, h],
            recv_sem=part_recv_sems.at[k - 1, h],
            device_id=resp_peer(k),
            device_id_type=MESH,
        )

    small_copies = [
        pltpu.make_async_copy(source, target, small_sems.at[i])
        for i, (source, target) in enumerate(
            (
                (rollout_hbm, rollout_ref),
                (destination_hbm, destination_ref),
                (base_hbm, base_ref),
            )
        )
    ]

    barrier = pltpu.get_barrier_semaphore()
    for k in range(1, n_resp):
        pl.semaphore_signal(barrier, inc=1, device_id=resp_peer(k), device_id_type=MESH)
    for k in range(1, n_dp):
        pl.semaphore_signal(barrier, inc=1, device_id=dp_peer(k), device_id_type=MESH)
    for copy in small_copies:
        copy.start()
    for copy in own_copies:
        copy.start()
    for h in range(KVH):
        for copy in load_copies(h):
            copy.start()

    pl.semaphore_wait(barrier, n_resp - 1 + n_dp - 1)
    for h in range(KVH):
        for k in range(1, n_resp):
            for x in range(2):
                prefix_copy(k, h, x, my_resp).start()
    for copy in small_copies:
        copy.wait()
    row_send[...] = jnp.zeros_like(row_send)
    row_send[0:1, :] = rollout_ref[...]
    row_send[1:2, :] = destination_ref[...].astype(jnp.float32)
    for k in range(1, n_dp):
        row_copy(k).start()
    key_index = lax.broadcasted_iota(jnp.int32, (total, tok), 0)
    query_index = lax.broadcasted_iota(jnp.int32, (total, tok), 1)
    allowed = ((key_index < prefix_rows) & (key_index < blocks_ref[0, 0] * BLOCK)) | (
        (key_index >= prefix_rows) & (key_index - prefix_rows <= query_index)
    )
    bias_ref[...] = jnp.where(allowed, 0.0, -1e30)
    for copy in own_copies:
        copy.wait()

    def forward(h, gained):
        for copy in load_copies(h):
            copy.wait()
        for k in range(1, n_resp):
            for x in range(2):
                prefix_copy(k, h, x, lax.rem(my_resp + n_resp - k, n_resp)).wait_recv()
        keys = kv_ref[:, kv_cols(h, 0)]
        values = kv_ref[:, kv_cols(h, 1)]
        bias = jnp.concatenate([bias_ref[...]] * PAIR, axis=1)
        for g in range(0, GQ, PAIR):
            starts = [pl.multiple_of(h * width + (g + i) * HD, HD) for i in range(PAIR)]
            q_rows = jnp.concatenate([q_ref[:, pl.ds(s, HD)] for s in starts], axis=0)
            d_rows = jnp.concatenate([d_ref[:, pl.ds(s, HD)] for s in starts], axis=0)
            scores = dot(keys, q_rows, ((1,), (1,))) * (score_scale * math.log2(math.e)) + bias
            shifted = jnp.exp2(scores - jnp.max(scores, axis=0, keepdims=True))
            inverse = 1.0 / jnp.sum(shifted, axis=0, keepdims=True)
            prob = (shifted * inverse).astype(jnp.bfloat16)
            wide = prob.astype(jnp.float32)
            toward = dot(values, d_rows, ((1,), (1,)))
            delta = jnp.sum(wide * toward, axis=0, keepdims=True)
            cols = pl.ds(g * HD, PAIR * HD)
            prob_ref[h, :, cols] = prob
            core_ref[h, :, cols] = (wide * (toward - delta)).astype(jnp.bfloat16)
            for i in range(PAIR):
                gained = gained + delta[:, i * HD : (i + 1) * HD]
        return gained

    gained = lax.fori_loop(0, KVH, forward, jnp.zeros((1, tok), jnp.float32))

    slot = (lax.broadcasted_iota(jnp.int32, (tok, tok), 0) + my_dp * tok).astype(jnp.float32)
    placed = jnp.where(row_send[1:2, :] == slot, row_send[0:1, :], 0.0)
    for k in range(1, n_dp):
        row_copy(k).wait_recv()
        placed = placed + jnp.where(
            row_recv[k - 1, 1:2, :] == slot, row_recv[k - 1, 0:1, :], 0.0
        )
    old = jnp.sum(placed.T, axis=0, keepdims=True)
    ratio = jnp.clip(jnp.exp(base_ref[...] + gained - old), clip_lower, clip_upper)
    length = lengths_ref[0, 0]
    coeff = jnp.where(
        lax.broadcasted_iota(jnp.int32, (1, tok), 1) < length,
        (-loss_scale * ratio) * advantage_ref[0, 0] / length.astype(jnp.float32),
        0.0,
    )
    coeff_rows = jnp.broadcast_to(coeff, (tok, tok)).T

    def kv_backward(h, carry):
        starts = [pl.multiple_of(h * width + g * HD, HD) for g in range(GQ)]
        for x, source, weights, factor in (
            (0, q_ref, core_ref, coeff_rows * score_scale),
            (1, d_ref, prob_ref, coeff_rows),
        ):
            rows = jnp.concatenate(
                [
                    (source[:, pl.ds(s, HD)].astype(jnp.float32) * factor).astype(jnp.bfloat16)
                    for s in starts
                ],
                axis=0,
            )
            grad = dot(weights[h], rows, ((1,), (0,))).astype(jnp.bfloat16)
            for owner in range(n_resp):
                part_send[h, owner, x] = grad[owner * shard : (owner + 1) * shard]
            rg_ref[:, kv_cols(h, x)] = grad[prefix_rows:]
        for k in range(1, n_resp):
            part_copy(k, h).start()
        return carry

    lax.fori_loop(0, KVH, kv_backward, 0)

    def query_backward(h, carry):
        grad = dot(kv_ref[:, kv_cols(h, 0)], core_ref[h], ((0,), (0,)))
        for g in range(GQ):
            one = grad[:, g * HD : (g + 1) * HD] * (coeff * score_scale)
            start = pl.multiple_of(h * width + g * HD, HD)
            qg_ref[:, pl.ds(start, HD)] = one.T.astype(jnp.bfloat16)
        return carry

    lax.fori_loop(0, KVH, query_backward, 0)

    for h in range(KVH):
        for k in range(1, n_resp):
            part_copy(k, h).wait_recv()
        for x in range(2):
            summed = part_send[h, my_resp, x].astype(jnp.float32)
            for k in range(1, n_resp):
                summed = summed + part_recv[k - 1, h, x].astype(jnp.float32)
            pg_ref[:, kv_cols(h, x)] = summed.astype(jnp.bfloat16)

    for k in range(1, n_dp):
        row_copy(k).wait_send()
    for h in range(KVH):
        for k in range(1, n_resp):
            for x in range(2):
                prefix_copy(k, h, x, my_resp).wait_send()
            part_copy(k, h).wait_send()


def deliver(*refs):
    count = len(refs) // 2
    sems = refs[-1]
    copies = [
        pltpu.make_async_copy(refs[i], refs[count + i], sems.at[i]) for i in range(count)
    ]
    for copy in copies:
        copy.start()
    for copy in copies:
        copy.wait()


def body(
    queries,
    prefix_kv,
    resp_kv,
    direction,
    base_logprob,
    rollout_logprob,
    destination,
    advantage,
    lengths,
    prefix_blocks,
):
    n_dp, n_resp = lax.axis_size("dp"), lax.axis_size("resp")
    tok = queries.shape[2]
    shard, kv_width = prefix_kv.shape[1:]
    total = n_resp * shard + tok
    columns = QH * HD
    any_spec = pl.BlockSpec(memory_space=pl.ANY)
    vmem_spec = pl.BlockSpec(memory_space=pltpu.VMEM)
    smem_spec = pl.BlockSpec(memory_space=pltpu.SMEM)
    dma = pltpu.SemaphoreType.DMA
    bf16, f32 = jnp.bfloat16, jnp.float32
    grads = pl.pallas_call(
        functools.partial(kernel, n_dp, n_resp),
        out_shape=(
            pltpu.VMEM((tok, columns), bf16),
            pltpu.VMEM((tok, kv_width), bf16),
            pltpu.VMEM((shard, kv_width), bf16),
        ),
        in_specs=[any_spec] * 7 + [smem_spec] * 3,
        out_specs=(vmem_spec, vmem_spec, vmem_spec),
        scratch_shapes=[
            pltpu.VMEM((tok, columns), bf16),
            pltpu.VMEM((tok, columns), bf16),
            pltpu.VMEM((total, kv_width), bf16),
            pltpu.VMEM((KVH, total, GQ * tok), bf16),
            pltpu.VMEM((KVH, total, GQ * tok), bf16),
            pltpu.VMEM((total, tok), f32),
            pltpu.VMEM((8, tok), f32),
            pltpu.VMEM((n_dp - 1, 8, tok), f32),
            pltpu.VMEM((KVH, n_resp, 2, shard, HD), bf16),
            pltpu.VMEM((n_resp - 1, KVH, 2, shard, HD), bf16),
            dma((KVH, 2)),
            dma((2,)),
            dma((n_resp - 1, KVH, 2)),
            dma((n_resp - 1, KVH, 2)),
            dma((n_dp - 1,)),
            dma((n_dp - 1,)),
            dma((n_resp - 1, KVH)),
            dma((n_resp - 1, KVH)),
            pltpu.VMEM((1, tok), f32),
            pltpu.VMEM((1, tok), f32),
            pltpu.VMEM((1, tok), jnp.int32),
            dma((3,)),
        ],
        compiler_params=pltpu.CompilerParams(
            collective_id=0, has_side_effects=True, vmem_limit_bytes=56 << 20
        ),
    )(
        queries[0, 0],
        prefix_kv[0],
        resp_kv[0, 0],
        direction[0, 0],
        base_logprob[0],
        rollout_logprob[0],
        destination[0],
        advantage,
        lengths,
        prefix_blocks,
    )
    query_grad, resp_grad, prefix_grad = pl.pallas_call(
        deliver,
        out_shape=tuple(jax.ShapeDtypeStruct(g.shape, g.dtype) for g in grads),
        in_specs=[vmem_spec] * 3,
        out_specs=(any_spec, any_spec, any_spec),
        scratch_shapes=[dma((3,))],
    )(*[pltpu.with_memory_space_constraint(g, pltpu.VMEM) for g in grads])
    return query_grad[None, None], resp_grad[None, None], prefix_grad[None]


def solution(mesh):
    return jax.shard_map(
        body,
        mesh=mesh,
        in_specs=(
            P("dp", "resp", None, None),
            P("dp", "resp", None),
            P("dp", "resp", None, None),
            P("dp", "resp", None, None),
            P("dp", "resp", None),
            P("dp", "resp", None),
            P("dp", "resp", None),
            P("dp", "resp"),
            P("dp", "resp"),
            P("dp", "resp"),
        ),
        out_specs=(P("dp", "resp", None, None), P("dp", "resp", None, None), P("dp", "resp", None)),
        check_vma=False,
    )
```

```python
import functools
import math

import jax
import jax.numpy as jnp
from jax import lax
from jax.experimental import pallas as pl
from jax.experimental.pallas import tpu as pltpu
from jax.sharding import PartitionSpec as P

QH = 32
KVH = 4
HD = 128
GQ = 8
BLOCK = 128
PAIR = 4

loss_scale = 65536.0
clip_lower = 0.8
clip_upper = 1.28

MESH = pl.DeviceIdType.MESH


def dot(a, b, dims):
    return lax.dot_general(a, b, (dims, ((), ())), preferred_element_type=jnp.float32)


def kernel(
    n_dp,
    n_resp,
    queries_hbm,
    prefix_hbm,
    resp_hbm,
    direction_hbm,
    base_hbm,
    rollout_hbm,
    destination_hbm,
    advantage_ref,
    lengths_ref,
    blocks_ref,
    qg_ref,
    rg_ref,
    pg_ref,
    q_ref,
    d_ref,
    kv_ref,
    prob_ref,
    core_ref,
    bias_ref,
    row_send,
    row_recv,
    part_send,
    part_recv,
    load_sems,
    own_sems,
    prefix_send_sems,
    prefix_recv_sems,
    row_send_sems,
    row_recv_sems,
    part_send_sems,
    part_recv_sems,
    base_ref,
    rollout_ref,
    destination_ref,
    small_sems,
    rows_ref,
):
    my_dp, my_resp = lax.axis_index("dp"), lax.axis_index("resp")
    tok = q_ref.shape[0]
    shard = prefix_hbm.shape[0]
    total = kv_ref.shape[0]
    prefix_rows = total - tok
    width = GQ * HD
    score_scale = 1.0 / math.sqrt(HD)

    def head_cols(h):
        return pl.ds(pl.multiple_of(h * width, width), width)

    def kv_cols(h, x):
        return pl.ds(pl.multiple_of((x * KVH + h) * HD, HD), HD)

    def load_copies(h):
        return (
            pltpu.make_async_copy(
                queries_hbm.at[:, head_cols(h)], q_ref.at[:, head_cols(h)], load_sems.at[h, 0]
            ),
            pltpu.make_async_copy(
                direction_hbm.at[:, head_cols(h)], d_ref.at[:, head_cols(h)], load_sems.at[h, 1]
            ),
        )

    def shard_rows(owner):
        return pl.ds(pl.multiple_of(owner * shard, shard), shard)

    own_copies = (
        pltpu.make_async_copy(
            resp_hbm, kv_ref.at[pl.ds(prefix_rows, tok), :], own_sems.at[0]
        ),
        pltpu.make_async_copy(prefix_hbm, kv_ref.at[shard_rows(my_resp), :], own_sems.at[1]),
    )

    def resp_peer(k):
        return (my_dp, lax.rem(my_resp + k, n_resp))

    def dp_peer(k):
        return (lax.rem(my_dp + k, n_dp), my_resp)

    def prefix_copy(k, h, x, owner):
        return pltpu.make_async_remote_copy(
            src_ref=prefix_hbm.at[:, kv_cols(h, x)],
            dst_ref=kv_ref.at[shard_rows(owner), kv_cols(h, x)],
            send_sem=prefix_send_sems.at[k - 1, h, x],
            recv_sem=prefix_recv_sems.at[k - 1, h, x],
            device_id=resp_peer(k),
            device_id_type=MESH,
        )

    def row_copy(k):
        return pltpu.make_async_remote_copy(
            src_ref=row_send,
            dst_ref=row_recv.at[k - 1],
            send_sem=row_send_sems.at[k - 1],
            recv_sem=row_recv_sems.at[k - 1],
            device_id=dp_peer(k),
            device_id_type=MESH,
        )

    def part_copy(k, h):
        return pltpu.make_async_remote_copy(
            src_ref=part_send.at[h, lax.rem(my_resp + k, n_resp)],
            dst_ref=part_recv.at[k - 1, h],
            send_sem=part_send_sems.at[k - 1, h],
            recv_sem=part_recv_sems.at[k - 1, h],
            device_id=resp_peer(k),
            device_id_type=MESH,
        )

    small_copies = [
        pltpu.make_async_copy(source, target, small_sems.at[i])
        for i, (source, target) in enumerate(
            (
                (rollout_hbm, rollout_ref),
                (destination_hbm, destination_ref),
                (base_hbm, base_ref),
            )
        )
    ]

    barrier = pltpu.get_barrier_semaphore()
    for k in range(1, n_resp):
        pl.semaphore_signal(barrier, inc=1, device_id=resp_peer(k), device_id_type=MESH)
    for k in range(1, n_dp):
        pl.semaphore_signal(barrier, inc=1, device_id=dp_peer(k), device_id_type=MESH)
    for copy in small_copies:
        copy.start()
    for copy in own_copies:
        copy.start()
    for h in range(KVH):
        for copy in load_copies(h):
            copy.start()

    pl.semaphore_wait(barrier, n_resp - 1 + n_dp - 1)
    for h in range(KVH):
        for k in range(1, n_resp):
            for x in range(2):
                prefix_copy(k, h, x, my_resp).start()
    for copy in small_copies:
        copy.wait()
    row_send[...] = jnp.zeros_like(row_send)
    row_send[0:1, :] = rollout_ref[...]
    row_send[1:2, :] = destination_ref[...].astype(jnp.float32)
    for k in range(1, n_dp):
        row_copy(k).start()
    key_index = lax.broadcasted_iota(jnp.int32, (total, tok), 0)
    query_index = lax.broadcasted_iota(jnp.int32, (total, tok), 1)
    allowed = ((key_index < prefix_rows) & (key_index < blocks_ref[0, 0] * BLOCK)) | (
        (key_index >= prefix_rows) & (key_index - prefix_rows <= query_index)
    )
    bias_ref[...] = jnp.where(allowed, 0.0, -1e30)
    for copy in own_copies:
        copy.wait()

    def forward(h, gained):
        for copy in load_copies(h):
            copy.wait()
        for k in range(1, n_resp):
            for x in range(2):
                prefix_copy(k, h, x, lax.rem(my_resp + n_resp - k, n_resp)).wait_recv()
        keys = kv_ref[:, kv_cols(h, 0)]
        values = kv_ref[:, kv_cols(h, 1)]
        bias = jnp.concatenate([bias_ref[...]] * PAIR, axis=1)
        for g in range(0, GQ, PAIR):
            starts = [pl.multiple_of(h * width + (g + i) * HD, HD) for i in range(PAIR)]
            q_rows = jnp.concatenate([q_ref[:, pl.ds(s, HD)] for s in starts], axis=0)
            d_rows = jnp.concatenate([d_ref[:, pl.ds(s, HD)] for s in starts], axis=0)
            scores = dot(keys, q_rows, ((1,), (1,))) * (score_scale * math.log2(math.e)) + bias
            shifted = jnp.exp2(scores - jnp.max(scores, axis=0, keepdims=True))
            inverse = 1.0 / jnp.sum(shifted, axis=0, keepdims=True)
            prob = (shifted * inverse).astype(jnp.bfloat16)
            wide = prob.astype(jnp.float32)
            toward = dot(values, d_rows, ((1,), (1,)))
            delta = jnp.sum(wide * toward, axis=0, keepdims=True)
            cols = pl.ds(g * HD, PAIR * HD)
            prob_ref[h, :, cols] = prob
            core_ref[h, :, cols] = (wide * (toward - delta)).astype(jnp.bfloat16)
            for i in range(PAIR):
                gained = gained + delta[:, i * HD : (i + 1) * HD]
        return gained

    gained = lax.fori_loop(0, KVH, forward, jnp.zeros((1, tok), jnp.float32))

    slot = (lax.broadcasted_iota(jnp.int32, (tok, tok), 0) + my_dp * tok).astype(jnp.float32)
    placed = jnp.where(row_send[1:2, :] == slot, row_send[0:1, :], 0.0)
    for k in range(1, n_dp):
        row_copy(k).wait_recv()
        placed = placed + jnp.where(
            row_recv[k - 1, 1:2, :] == slot, row_recv[k - 1, 0:1, :], 0.0
        )
    old = jnp.sum(placed.T, axis=0, keepdims=True)
    ratio = jnp.clip(jnp.exp(base_ref[...] + gained - old), clip_lower, clip_upper)
    length = lengths_ref[0, 0]
    coeff = jnp.where(
        lax.broadcasted_iota(jnp.int32, (1, tok), 1) < length,
        (-loss_scale * ratio) * advantage_ref[0, 0] / length.astype(jnp.float32),
        0.0,
    )
    coeff_rows = jnp.broadcast_to(coeff, (tok, tok)).T

    def kv_backward(h, carry):
        starts = [pl.multiple_of(h * width + g * HD, HD) for g in range(GQ)]
        for x, source, weights, factor in (
            (0, q_ref, core_ref, coeff_rows * score_scale),
            (1, d_ref, prob_ref, coeff_rows),
        ):
            rows = jnp.concatenate(
                [
                    (source[:, pl.ds(s, HD)].astype(jnp.float32) * factor).astype(jnp.bfloat16)
                    for s in starts
                ],
                axis=0,
            )
            rows_ref[h, x] = rows
            grad = dot(weights[h, :prefix_rows], rows, ((1,), (0,))).astype(jnp.bfloat16)
            for owner in range(n_resp):
                part_send[h, owner, x] = grad[owner * shard : (owner + 1) * shard]
        for k in range(1, n_resp):
            part_copy(k, h).start()
        return carry

    lax.fori_loop(0, KVH, kv_backward, 0)

    def query_backward(h, carry):
        grad = dot(kv_ref[:, kv_cols(h, 0)], core_ref[h], ((0,), (0,)))
        for g in range(GQ):
            one = grad[:, g * HD : (g + 1) * HD] * (coeff * score_scale)
            start = pl.multiple_of(h * width + g * HD, HD)
            qg_ref[:, pl.ds(start, HD)] = one.T.astype(jnp.bfloat16)
        for x, weights in ((0, core_ref), (1, prob_ref)):
            own = dot(weights[h, prefix_rows:], rows_ref[h, x], ((1,), (0,)))
            rg_ref[:, kv_cols(h, x)] = own.astype(jnp.bfloat16)
        return carry

    lax.fori_loop(0, KVH, query_backward, 0)

    for h in range(KVH):
        for k in range(1, n_resp):
            part_copy(k, h).wait_recv()
        for x in range(2):
            summed = part_send[h, my_resp, x].astype(jnp.float32)
            for k in range(1, n_resp):
                summed = summed + part_recv[k - 1, h, x].astype(jnp.float32)
            pg_ref[:, kv_cols(h, x)] = summed.astype(jnp.bfloat16)

    for k in range(1, n_dp):
        row_copy(k).wait_send()
    for h in range(KVH):
        for k in range(1, n_resp):
            for x in range(2):
                prefix_copy(k, h, x, my_resp).wait_send()
            part_copy(k, h).wait_send()


def deliver(*refs):
    count = len(refs) // 2
    sems = refs[-1]
    copies = [
        pltpu.make_async_copy(refs[i], refs[count + i], sems.at[i]) for i in range(count)
    ]
    for copy in copies:
        copy.start()
    for copy in copies:
        copy.wait()


def body(
    queries,
    prefix_kv,
    resp_kv,
    direction,
    base_logprob,
    rollout_logprob,
    destination,
    advantage,
    lengths,
    prefix_blocks,
):
    n_dp, n_resp = lax.axis_size("dp"), lax.axis_size("resp")
    tok = queries.shape[2]
    shard, kv_width = prefix_kv.shape[1:]
    total = n_resp * shard + tok
    columns = QH * HD
    any_spec = pl.BlockSpec(memory_space=pl.ANY)
    vmem_spec = pl.BlockSpec(memory_space=pltpu.VMEM)
    smem_spec = pl.BlockSpec(memory_space=pltpu.SMEM)
    dma = pltpu.SemaphoreType.DMA
    bf16, f32 = jnp.bfloat16, jnp.float32
    grads = pl.pallas_call(
        functools.partial(kernel, n_dp, n_resp),
        out_shape=(
            pltpu.VMEM((tok, columns), bf16),
            pltpu.VMEM((tok, kv_width), bf16),
            pltpu.VMEM((shard, kv_width), bf16),
        ),
        in_specs=[any_spec] * 7 + [smem_spec] * 3,
        out_specs=(vmem_spec, vmem_spec, vmem_spec),
        scratch_shapes=[
            pltpu.VMEM((tok, columns), bf16),
            pltpu.VMEM((tok, columns), bf16),
            pltpu.VMEM((total, kv_width), bf16),
            pltpu.VMEM((KVH, total, GQ * tok), bf16),
            pltpu.VMEM((KVH, total, GQ * tok), bf16),
            pltpu.VMEM((total, tok), f32),
            pltpu.VMEM((8, tok), f32),
            pltpu.VMEM((n_dp - 1, 8, tok), f32),
            pltpu.VMEM((KVH, n_resp, 2, shard, HD), bf16),
            pltpu.VMEM((n_resp - 1, KVH, 2, shard, HD), bf16),
            dma((KVH, 2)),
            dma((2,)),
            dma((n_resp - 1, KVH, 2)),
            dma((n_resp - 1, KVH, 2)),
            dma((n_dp - 1,)),
            dma((n_dp - 1,)),
            dma((n_resp - 1, KVH)),
            dma((n_resp - 1, KVH)),
            pltpu.VMEM((1, tok), f32),
            pltpu.VMEM((1, tok), f32),
            pltpu.VMEM((1, tok), jnp.int32),
            dma((3,)),
            pltpu.VMEM((KVH, 2, GQ * tok, HD), bf16),
        ],
        compiler_params=pltpu.CompilerParams(
            collective_id=0, has_side_effects=True, vmem_limit_bytes=56 << 20
        ),
    )(
        queries[0, 0],
        prefix_kv[0],
        resp_kv[0, 0],
        direction[0, 0],
        base_logprob[0],
        rollout_logprob[0],
        destination[0],
        advantage,
        lengths,
        prefix_blocks,
    )
    query_grad, resp_grad, prefix_grad = pl.pallas_call(
        deliver,
        out_shape=tuple(jax.ShapeDtypeStruct(g.shape, g.dtype) for g in grads),
        in_specs=[vmem_spec] * 3,
        out_specs=(any_spec, any_spec, any_spec),
        scratch_shapes=[dma((3,))],
    )(*[pltpu.with_memory_space_constraint(g, pltpu.VMEM) for g in grads])
    return query_grad[None, None], resp_grad[None, None], prefix_grad[None]


def solution(mesh):
    return jax.shard_map(
        body,
        mesh=mesh,
        in_specs=(
            P("dp", "resp", None, None),
            P("dp", "resp", None),
            P("dp", "resp", None, None),
            P("dp", "resp", None, None),
            P("dp", "resp", None),
            P("dp", "resp", None),
            P("dp", "resp", None),
            P("dp", "resp"),
            P("dp", "resp"),
            P("dp", "resp"),
        ),
        out_specs=(P("dp", "resp", None, None), P("dp", "resp", None, None), P("dp", "resp", None)),
        check_vma=False,
    )
```
